128 devices in a mesh: trial: 2 (over core), tmpl: 64 (over z, x, y).
Axes of the slice: x: 4, y: 4, z: 4, core: 2. Of those that a mesh axis runs over, the one named last changes fastest.
Arguments:
- spectra: bfloat16 [2, 2, 64, 2, 16896], P(None, 'trial', 'tmpl'), may hold values from -6 to 6
- half_spectra: bfloat16 [2, 2, 64, 2, 8704], P(None, 'trial', 'tmpl'), may hold values from -6 to 6
- kernels: bfloat16 [1024, 2, 512], P('tmpl'), may hold values from -0.1875 to 0.1875
- owners: int32 [2, 2], replicated, may hold values from 0 to 127, as said below
- counts: int32 [64], replicated, may hold values from 12 to 16, as said below
- partners: int32 [1024], replicated, may hold values from -1 to 1023, as said below
Outputs:
- powers: bfloat16 [2, 2, 1024, 16384], P(None, 'trial', 'tmpl')
The draws below stay inside these ranges and needn't reach their ends.
Inputs may be any that keep to these rules, and one draw needn't show every extreme that they name: owners[w, t] = i * 64 + c names the device with trial index i and tmpl index c that holds window w's data of trial t; the two trials of a window lie on different trial indices, and the trial index holding trial 0 alternates from one window to the next; in some window the two trials lie on devices 0 and 127. The live templates of tmpl index d are its first counts[d]; some index has all 16 live. For a live template j, partners[j] is a live template; the live templates of one tmpl index name templates of any one tmpl index at most 1 times, and some index does so exactly 1 times; partners[j] = -1 for every template that is not live.
All inputs are finite; a program needn't handle non-finite values.
Results may differ from the reference program's by a relative error of at most 0.004.
Values may be sent and summed in bfloat16 or wider, within the bound.
No kernel may reach another device: no remote copies, remote signals or barrier semaphores. Data moves between devices by JAX's collectives and lax.ppermute only.
A program may use at most 128 MiB of HBM per device.

```python
import jax
import jax.numpy as jnp

BINS = 16384
TAPS = 512
TMPL_DEV = 16
WINDOWS = 2
HALF_BINS = 8192
SLAB = 16896
HALF_SLAB = 8704
TEMPLATES = 1024
CAPACITY = 1
N_TRIAL = 2
N_TMPL = 64


def live_counts(key):
    devices_count = TEMPLATES // TMPL_DEV
    lowest = max(1, 3 * TMPL_DEV // 4)
    drawn_counts = jax.random.randint(jax.random.fold_in(key, 101), (devices_count,), lowest, TMPL_DEV + 1)
    filled = jax.random.randint(jax.random.fold_in(key, 102), (), 0, devices_count)
    return jnp.where(jnp.arange(devices_count) == filled, TMPL_DEV, drawn_counts).astype(jnp.int32)


def draw_counts(key, part):
    return live_counts(key)


def draw_partners(key, part):
    devices_count = TEMPLATES // TMPL_DEV
    counts = live_counts(key)
    slot_total = CAPACITY * devices_count
    noise_int = jax.random.randint(jax.random.fold_in(key, 201), (devices_count, slot_total), 0, 2 ** 20)
    favour = jax.random.randint(jax.random.fold_in(key, 202), (devices_count,), 0, 2 ** 20)
    lane_ids = jnp.arange(slot_total, dtype=jnp.int32)
    scores = (noise_int + favour[lane_ids // CAPACITY][None, :]) * slot_total + lane_ids[None, :]
    ordering = jnp.argsort(-scores, axis=1, stable=True)[:, :TMPL_DEV]
    holders = (ordering // CAPACITY).astype(jnp.int32)
    within = jax.random.randint(jax.random.fold_in(key, 203), (devices_count, TMPL_DEV), 0, counts[holders])
    chosen = holders * TMPL_DEV + within
    live_mask = jnp.arange(TMPL_DEV)[None, :] < counts[:, None]
    return jnp.where(live_mask, chosen, -1).reshape(TEMPLATES).astype(jnp.int32)


def draw_owners(key, part):
    devices_count = TEMPLATES // TMPL_DEV
    phase_bit = jax.random.randint(jax.random.fold_in(key, 301), (), 0, 2)
    first_row = (jnp.arange(WINDOWS, dtype=jnp.int32) + phase_bit) % 2
    row_pick = jnp.stack([first_row, 1 - first_row], axis=1)
    columns = jax.random.randint(jax.random.fold_in(key, 302), (WINDOWS, 2), 0, devices_count)
    extreme_window = jax.random.randint(jax.random.fold_in(key, 303), (), 0, WINDOWS)
    extreme_columns = jnp.where(row_pick == 0, 0, devices_count - 1)
    is_extreme = (jnp.arange(WINDOWS, dtype=jnp.int32) == extreme_window)[:, None]
    columns = jnp.where(is_extreme, extreme_columns, columns)
    return (row_pick * devices_count + columns).astype(jnp.int32)


def level_of(rng, extent, cuts, low, largest):
    level, own = 1.0, jax.random.fold_in(rng, 6)
    for position, blocks in cuts:
        heights = jnp.exp(jax.random.uniform(jax.random.fold_in(own, position), (blocks,), jnp.float32, low / len(cuts), largest / len(cuts)))
        level = level * jnp.repeat(heights, extent[position] // blocks).reshape([-1 if axis == position else 1 for axis in range(len(extent))])
    return level


def scatter_about(rng, shape, scale, most, split=(), kind=jnp.bfloat16):
    factor_of = level_of(rng, shape, split, -0.22, 0.18) if split else 1.0
    drawn = jax.random.normal(rng, shape, jnp.float32) * scale * factor_of
    return jnp.minimum(jnp.maximum(drawn, -most), most).astype(kind)


def setup_inputs(seed: int = 0) -> dict:
    arg_keys = jax.random.split(jax.random.key(seed), 7)
    spectra = scatter_about(arg_keys[0], (WINDOWS, N_TRIAL, N_TMPL, 2, SLAB), 1.0, 6.0, ((1, 2), (2, 64)))
    half_spectra = scatter_about(arg_keys[1], (WINDOWS, N_TRIAL, N_TMPL, 2, HALF_SLAB), 1.0, 6.0, ((1, 2), (2, 64)))
    kernels = scatter_about(arg_keys[2], (TEMPLATES, 2, TAPS), (2 * TAPS) ** -0.5, 0.1875, ((0, 64),))
    owners = draw_owners(jax.random.fold_in(arg_keys[6], 71), 0)
    counts = draw_counts(jax.random.fold_in(arg_keys[6], 71), 0)
    partners = draw_partners(jax.random.fold_in(arg_keys[6], 71), 0)
    return {"spectra": spectra, "half_spectra": half_spectra, "kernels": kernels, "owners": owners, "counts": counts, "partners": partners}


def hankel_rows(signal, tap_count, columns):
    length = signal.shape[1]
    repeated = jnp.broadcast_to(signal[:, None, :], (2, tap_count + 1, length)).reshape(2, (tap_count + 1) * length)
    skewed = repeated[:, : tap_count * (length + 1)].reshape(2, tap_count, length + 1)
    return skewed[:, :, :columns].reshape(2 * tap_count, columns)


def kernel_matrix(kernel_set):
    real_part = kernel_set[:, 0, :]
    imag_part = kernel_set[:, 1, :]
    upper_rows = jnp.concatenate([real_part, -imag_part], axis=1)
    lower_rows = jnp.concatenate([imag_part, real_part], axis=1)
    return jnp.concatenate([upper_rows, lower_rows], axis=0)


def power_rows(weights, stacked):
    product = jnp.dot(weights, stacked, preferred_element_type=jnp.float32)
    middle = weights.shape[0] // 2
    return product[:middle] * product[:middle] + product[middle:] * product[middle:]


def reference(spectra, half_spectra, kernels, owners, counts, partners):
    weights = kernel_matrix(kernels)
    indices = jnp.arange(TEMPLATES, dtype=jnp.int32)
    live_mask = (indices % TMPL_DEV) < counts[indices // TMPL_DEV]
    sources = jnp.maximum(partners, 0)
    windows_out = []
    for window in range(WINDOWS):
        trials_out = []
        for trial_index in range(N_TRIAL):
            owner_id = owners[window, trial_index]
            whole_slab = spectra[window, owner_id // N_TMPL, owner_id % N_TMPL]
            halved = half_spectra[window, owner_id // N_TMPL, owner_id % N_TMPL]
            direct = power_rows(weights, hankel_rows(whole_slab, TAPS, BINS))
            planes = power_rows(weights, hankel_rows(halved, TAPS, HALF_BINS)).astype(jnp.bfloat16)
            borrowed = jnp.repeat(planes[sources], 2, axis=1).astype(jnp.float32)
            summed = jnp.where(live_mask[:, None], direct + borrowed, jnp.float32(0.0))
            trials_out.append(summed.astype(jnp.bfloat16))
        windows_out.append(jnp.stack(trials_out))
    return jnp.stack(windows_out)
```

```python
import jax
import jax.numpy as jnp
from jax import lax
from jax.experimental import pallas as pl
from jax.experimental.pallas import tpu as pltpu
from jax.sharding import Mesh
from jax.sharding import PartitionSpec as P

TMPL = ("tmpl_0", "tmpl_1", "tmpl_2")
F32 = jnp.float32
BF = jnp.bfloat16
VMEM = pl.BlockSpec(memory_space=pltpu.VMEM)
SMEM = pl.BlockSpec(memory_space=pltpu.SMEM)


def swapped(x):
    return lax.ppermute(x, "trial", [(0, 1), (1, 0)])


def pack_kernel(owners_ref, part_ref, k_ref, x_ref, y_ref, xc_ref, yc_ref, op_ref, rev_ref):
    me = lax.axis_index(TMPL)
    r0 = lax.broadcasted_iota(jnp.int32, (128, 128), 0)
    c0 = lax.broadcasted_iota(jnp.int32, (128, 128), 1)
    flip = (r0 == (128 - c0) % 128).astype(BF)
    rev = jnp.dot(k_ref[...], flip, preferred_element_type=F32).astype(BF)
    rev_ref[...] = rev
    wanted = jnp.concatenate(
        [
            (jnp.broadcast_to(part_ref[r : r + 1, :], (128, 128)) == me * 16 + r0 // 8).astype(BF)
            for r in range(8)
        ],
        axis=0,
    )
    group = (
        lax.broadcasted_iota(jnp.int32, (64, 128), 0) // 8
        == lax.broadcasted_iota(jnp.int32, (64, 128), 1) // 16
    ).astype(BF)
    hit = lax.dot_general(group, wanted, (((1,), (1,)), ((), ())), preferred_element_type=F32)
    same = (
        lax.broadcasted_iota(jnp.int32, (64, 128), 0) % 8
        == lax.broadcasted_iota(jnp.int32, (64, 128), 1) % 8
    )
    for r in range(8):
        pick = jnp.where(same, hit[:, r * 128 : (r + 1) * 128], 0.0).astype(BF)
        sent = jnp.dot(pick, rev, preferred_element_type=F32)
        op_ref[8 * r : 8 * r + 8, 0:8, :] = sent.reshape(8, 8, 128).astype(BF)
    op_ref[50:64, 8:24, :] = jnp.zeros((14, 16, 128), BF)
    for w in range(2):
        rows = slice(8 + 8 * w, 16 + 8 * w)
        crossed = owners_ref[w, 0] >= 64

        @pl.when(crossed)
        def _():
            op_ref[0:33, rows, :] = xc_ref[w]
            op_ref[33:50, rows, :] = yc_ref[w]

        @pl.when(jnp.logical_not(crossed))
        def _():
            op_ref[0:33, rows, :] = x_ref[w]
            op_ref[33:50, rows, :] = y_ref[w]


def relay_kernel(owners_ref, part_ref, got_ref, out_ref, h_ref):
    me = lax.axis_index(TMPL)
    row = lax.axis_index("trial")
    for w in range(2):
        block = got_ref[owners_ref[w, row] % 64, 8 + 8 * w : 16 + 8 * w, :]
        out_ref[:, 8 * w : 8 * w + 8, :] = jnp.broadcast_to(block[None], (64, 8, 128))
    for s in range(16):
        source = jnp.maximum(part_ref[me * 16 + s], 0) // 16
        h_ref[s] = got_ref[source, 0:8, :]


def correlate_kernel(counts_ref, g_ref, rev_ref, hrev_ref, out_ref, flat, y64, lx, ly, revf, hrevf, ra, rb, pa, pb, scr):
    me = lax.axis_index(TMPL)
    L=128
    for w in range(2):
        flat[w] = g_ref[:, 8*w:8*w+8, :].astype(F32).reshape(512, L)
    revf[...] = rev_ref[...].astype(F32)
    hrevf[...] = hrev_ref[...].astype(F32)
    lane=lax.broadcasted_iota(jnp.int32,(68,L),1)
    for w in range(2):
        for c in range(2):
            for q in range(5):
                lx[w*128:(w+1)*128, (c*5+q)*L:(c*5+q+1)*L] = flat[w, pl.ds(2*q+c,128,stride=2), :].astype(BF)
            even = flat[w, pl.ds(264+c,68,stride=2), :]
            nxt = flat[w, pl.ds(266+c,68,stride=2), :]
            odd = jnp.where(lane<64, pltpu.roll(even,64,1), pltpu.roll(nxt,64,1))
            y64[pl.ds(0,68,stride=2), :] = even
            y64[pl.ds(1,68,stride=2), :] = odd
            for q in range(5):
                ly[w*128:(w+1)*128, (c*5+q)*L:(c*5+q+1)*L] = y64[2*q:2*q+128, :].astype(BF)
    tri = lax.broadcasted_iota(jnp.int32,(L,L),0) >= lax.broadcasted_iota(jnp.int32,(L,L),1)
    left = lax.broadcasted_iota(jnp.int32,(L,L),1) < 64
    zero = jnp.zeros((L,L),F32)
    live_n = counts_ref[me]
    def circ(ref, row):
        v = jnp.broadcast_to(ref[pl.ds(row,1), :], (L,L))
        return pltpu.roll(v, 0, 1, stride=1, stride_axis=0)
    def tiles(cs):
        return [jnp.where(tri,cs[0],zero)]+[jnp.where(tri,cs[q],cs[q-1]) for q in (1,2,3)]+[jnp.where(tri,zero,cs[3])]
    def put(dst, re, im):
        for q in range(5):
            r = re[q].astype(BF); i = im[q].astype(BF)
            dst[q*L:(q+1)*L, 0:L] = r
            dst[q*L:(q+1)*L, L:2*L] = i
            dst[(5+q)*L:(6+q)*L, 0:L] = -i
            dst[(5+q)*L:(6+q)*L, L:2*L] = r
    def build(pair, r_refs, p_ref):
        for k in range(2):
            t = 2*pair+k
            put(r_refs[k], *[tiles([circ(revf, t*8+2*q+c) for q in range(4)]) for c in range(2)])
        h=[]
        for c in range(2):
            a = [circ(hrevf, (2*pair)*8+2*q+c) for q in range(4)]
            bb = [pltpu.roll(jnp.broadcast_to(hrevf[pl.ds((2*pair+1)*8+2*q+c,1), :],(L,L)),64,1,stride=1,stride_axis=0) for q in range(4)]
            m = [jnp.where(left, a[q], bb[q]) for q in range(4)]
            trc = lax.broadcasted_iota(jnp.int32,(L,L),0) >= lax.broadcasted_iota(jnp.int32,(L,L),1) % 64
            h.append([jnp.where(trc,m[0],zero)]+[jnp.where(trc,m[q],m[q-1]) for q in (1,2,3)]+[jnp.where(trc,zero,m[3])])
        put(p_ref, *h)
    er = lax.broadcasted_iota(jnp.int32,(L,2*L),0); ec = lax.broadcasted_iota(jnp.int32,(L,2*L),1)
    dup = (er == (ec//128)*64 + (ec%128)//2).astype(BF)
    def work(pair, r_refs, p_ref):
        z = jnp.dot(ly[...], p_ref[...], preferred_element_type=F32)
        plane = (z[:, :L]*z[:, :L] + z[:, L:]*z[:, L:]).astype(BF)
        wide = jnp.dot(plane, dup, preferred_element_type=F32)
        for k in range(2):
            t = 2*pair+k
            d = jnp.dot(lx[...], r_refs[k][...], preferred_element_type=F32)
            tot = d[:, :L]*d[:, :L] + d[:, L:]*d[:, L:] + wide[:, k*L:(k+1)*L]
            tot = jnp.where(t < live_n, tot, 0.0)
            scr[:, pl.ds(t,1), :] = tot.reshape(256,1,L)
    A=((ra.at[0],ra.at[1]),pa); B=((rb.at[0],rb.at[1]),pb)
    build(0,*A)
    def step(i,_):
        work(2*i,*A); build(2*i+1,*B)
        work(2*i+1,*B); build(jnp.minimum(2*i+2,7),*A)
        return 0
    lax.fori_loop(0,4,step,0)
    for w in range(2):
        def pk(a,_):
            out_ref[w, :, pl.ds(pl.multiple_of(a*L,L),L)] = scr[w*128+a].astype(BF)
            return 0
        lax.fori_loop(0,128,pk,0,unroll=8)


def body(spectra, half_spectra, kernels, owners, counts, partners):
    x = spectra.reshape(2, 2, 132, 128).transpose(0, 2, 1, 3).reshape(2, 33, 8, 128)
    y = half_spectra.reshape(2, 2, 68, 128).transpose(0, 2, 1, 3).reshape(2, 17, 8, 128)
    k = kernels.reshape(16, 2, 4, 128).transpose(0, 2, 1, 3).reshape(128, 128)
    xc, yc = swapped(x), swapped(y)
    sent, rev = pl.pallas_call(
        pack_kernel,
        out_shape=(
            jax.ShapeDtypeStruct((64, 24, 128), BF),
            jax.ShapeDtypeStruct((128, 128), BF),
        ),
        in_specs=[SMEM] + [VMEM] * 6,
        out_specs=(VMEM, VMEM),
        name="pack",
    )(owners, partners.reshape(8, 128), k, x, y, xc, yc)
    got = lax.all_to_all(sent, TMPL, 0, 0, tiled=True)
    repeated, h = pl.pallas_call(
        relay_kernel,
        out_shape=(
            jax.ShapeDtypeStruct((64, 16, 128), BF),
            jax.ShapeDtypeStruct((16, 8, 128), BF),
        ),
        in_specs=[SMEM, SMEM, VMEM],
        out_specs=(VMEM, VMEM),
        name="relay",
    )(owners, partners, got)
    whole = lax.all_to_all(repeated, TMPL, 0, 0, tiled=True)
    out = pl.pallas_call(
        correlate_kernel,
        out_shape=jax.ShapeDtypeStruct((2, 16, 16384), BF),
        in_specs=[SMEM] + [VMEM] * 3,
        out_specs=VMEM,
        scratch_shapes=[
            pltpu.VMEM((2, 512, 128), F32),
            pltpu.VMEM((136, 128), F32),
            pltpu.VMEM((256, 1280), BF),
            pltpu.VMEM((256, 1280), BF),
            pltpu.VMEM((128, 128), F32),
            pltpu.VMEM((128, 128), F32),
            pltpu.VMEM((2, 1280, 256), BF),
            pltpu.VMEM((2, 1280, 256), BF),
            pltpu.VMEM((1280, 256), BF),
            pltpu.VMEM((1280, 256), BF),
            pltpu.VMEM((256, 16, 128), F32),
        ],
        name="correlate",
    )(counts, whole, rev, h.reshape(128, 128))
    return out[:, None]


def solution(mesh):
    finer = Mesh(
        mesh.devices.reshape(mesh.shape["trial"], 4, 4, 4), ("trial", "tmpl_0", "tmpl_1", "tmpl_2")
    )
    in_specs = (
        P(None, "trial", TMPL, None, None),
        P(None, "trial", TMPL, None, None),
        P(TMPL, None, None),
        P(),
        P(),
        P(),
    )
    out_specs = P(None, "trial", TMPL, None)
    return jax.shard_map(body, mesh=finer, in_specs=in_specs, out_specs=out_specs, check_vma=False)
```

```python
import jax
import jax.numpy as jnp
from jax import lax
from jax.experimental import pallas as pl
from jax.experimental.pallas import tpu as pltpu
from jax.sharding import Mesh
from jax.sharding import PartitionSpec as P

TMPL = ("tmpl_0", "tmpl_1", "tmpl_2")
F32 = jnp.float32
BF = jnp.bfloat16
VMEM = pl.BlockSpec(memory_space=pltpu.VMEM)
SMEM = pl.BlockSpec(memory_space=pltpu.SMEM)


def swapped(x):
    return lax.ppermute(x, "trial", [(0, 1), (1, 0)])


def pack_kernel(owners_ref, part_ref, k_ref, x_ref, y_ref, xc_ref, yc_ref, op_ref, rev_ref):
    me = lax.axis_index(TMPL)
    r0 = lax.broadcasted_iota(jnp.int32, (128, 128), 0)
    c0 = lax.broadcasted_iota(jnp.int32, (128, 128), 1)
    flip = (r0 == (128 - c0) % 128).astype(BF)
    rev = jnp.dot(k_ref[...], flip, preferred_element_type=F32).astype(BF)
    rev_ref[...] = rev
    wanted = jnp.concatenate(
        [
            (jnp.broadcast_to(part_ref[r : r + 1, :], (128, 128)) == me * 16 + r0 // 8).astype(BF)
            for r in range(8)
        ],
        axis=0,
    )
    group = (
        lax.broadcasted_iota(jnp.int32, (64, 128), 0) // 8
        == lax.broadcasted_iota(jnp.int32, (64, 128), 1) // 16
    ).astype(BF)
    hit = lax.dot_general(group, wanted, (((1,), (1,)), ((), ())), preferred_element_type=F32)
    same = (
        lax.broadcasted_iota(jnp.int32, (64, 128), 0) % 8
        == lax.broadcasted_iota(jnp.int32, (64, 128), 1) % 8
    )
    for r in range(8):
        pick = jnp.where(same, hit[:, r * 128 : (r + 1) * 128], 0.0).astype(BF)
        sent = jnp.dot(pick, rev, preferred_element_type=F32)
        op_ref[8 * r : 8 * r + 8, 0:8, :] = sent.reshape(8, 8, 128).astype(BF)
    op_ref[50:64, 8:24, :] = jnp.zeros((14, 16, 128), BF)
    for w in range(2):
        rows = slice(8 + 8 * w, 16 + 8 * w)
        crossed = owners_ref[w, 0] >= 64

        @pl.when(crossed)
        def _():
            op_ref[0:33, rows, :] = xc_ref[w]
            op_ref[33:50, rows, :] = yc_ref[w]

        @pl.when(jnp.logical_not(crossed))
        def _():
            op_ref[0:33, rows, :] = x_ref[w]
            op_ref[33:50, rows, :] = y_ref[w]


def relay_kernel(owners_ref, part_ref, got_ref, out_ref, h_ref):
    me = lax.axis_index(TMPL)
    row = lax.axis_index("trial")
    for w in range(2):
        block = got_ref[owners_ref[w, row] % 64, 8 + 8 * w : 16 + 8 * w, :]
        out_ref[:, 8 * w : 8 * w + 8, :] = jnp.broadcast_to(block[None], (64, 8, 128))
    for s in range(16):
        source = jnp.maximum(part_ref[me * 16 + s], 0) // 16
        h_ref[s] = got_ref[source, 0:8, :]


def correlate_kernel(counts_ref, g_ref, rev_ref, hrev_ref, out_ref, flat, y64, lx, ly, revf, hrevf, ra, rb, pa, pb, scr):
    me = lax.axis_index(TMPL)
    L=128
    for w in range(2):
        flat[w] = g_ref[:, 8*w:8*w+8, :].astype(F32).reshape(512, L)
    revf[...] = rev_ref[...].astype(F32)
    hrevf[...] = hrev_ref[...].astype(F32)
    lane=lax.broadcasted_iota(jnp.int32,(68,L),1)
    for w in range(2):
        for c in range(2):
            for q in range(5):
                lx[w*128:(w+1)*128, (c*5+q)*L:(c*5+q+1)*L] = flat[w, pl.ds(2*q+c,128,stride=2), :].astype(BF)
            even = flat[w, pl.ds(264+c,68,stride=2), :]
            nxt = flat[w, pl.ds(266+c,68,stride=2), :]
            odd = jnp.where(lane<64, pltpu.roll(even,64,1), pltpu.roll(nxt,64,1))
            y64[pl.ds(0,68,stride=2), :] = even
            y64[pl.ds(1,68,stride=2), :] = odd
            for q in range(5):
                ly[w*128:(w+1)*128, (c*5+q)*L:(c*5+q+1)*L] = y64[2*q:2*q+128, :].astype(BF)
    tri = lax.broadcasted_iota(jnp.int32,(L,L),0) >= lax.broadcasted_iota(jnp.int32,(L,L),1)
    left = lax.broadcasted_iota(jnp.int32,(L,L),1) < 64
    zero = jnp.zeros((L,L),F32)
    live_n = counts_ref[me]
    def circ(ref, row):
        v = jnp.broadcast_to(ref[pl.ds(row,1), :], (L,L))
        return pltpu.roll(v, 0, 1, stride=1, stride_axis=0)
    def tiles(cs):
        return [jnp.where(tri,cs[0],zero)]+[jnp.where(tri,cs[q],cs[q-1]) for q in (1,2,3)]+[jnp.where(tri,zero,cs[3])]
    def put(dst, re, im):
        for q in range(5):
            r = re[q].astype(BF); i = im[q].astype(BF)
            dst[q*L:(q+1)*L, 0:L] = r
            dst[q*L:(q+1)*L, L:2*L] = i
            dst[(5+q)*L:(6+q)*L, 0:L] = -i
            dst[(5+q)*L:(6+q)*L, L:2*L] = r
    def build(pair, r_refs, p_ref):
        for k in range(2):
            t = 2*pair+k
            put(r_refs[k], *[tiles([circ(revf, t*8+2*q+c) for q in range(4)]) for c in range(2)])
        h=[]
        for c in range(2):
            a = [circ(hrevf, (2*pair)*8+2*q+c) for q in range(4)]
            bb = [pltpu.roll(jnp.broadcast_to(hrevf[pl.ds((2*pair+1)*8+2*q+c,1), :],(L,L)),64,1,stride=1,stride_axis=0) for q in range(4)]
            m = [jnp.where(left, a[q], bb[q]) for q in range(4)]
            trc = lax.broadcasted_iota(jnp.int32,(L,L),0) >= lax.broadcasted_iota(jnp.int32,(L,L),1) % 64
            h.append([jnp.where(trc,m[0],zero)]+[jnp.where(trc,m[q],m[q-1]) for q in (1,2,3)]+[jnp.where(trc,zero,m[3])])
        put(p_ref, *h)
    er = lax.broadcasted_iota(jnp.int32,(L,2*L),0); ec = lax.broadcasted_iota(jnp.int32,(L,2*L),1)
    dup = (er == (ec//128)*64 + (ec%128)//2).astype(BF)
    def work(pair, r_refs, p_ref):
        z = jnp.dot(ly[...], p_ref[...], preferred_element_type=F32)
        plane = (z[:, :L]*z[:, :L] + z[:, L:]*z[:, L:]).astype(BF)
        wide = jnp.dot(plane, dup, preferred_element_type=F32)
        for k in range(2):
            t = 2*pair+k
            d = jnp.dot(lx[...], r_refs[k][...], preferred_element_type=F32)
            tot = d[:, :L]*d[:, :L] + d[:, L:]*d[:, L:] + wide[:, k*L:(k+1)*L]
            tot = jnp.where(t < live_n, tot, 0.0)
            scr[:, pl.ds(t,1), :] = tot.reshape(256,1,L)
    A=((ra.at[0],ra.at[1]),pa); B=((rb.at[0],rb.at[1]),pb)
    build(0,*A)
    def step(i,_):
        work(2*i,*A); build(2*i+1,*B)
        work(2*i+1,*B); build(jnp.minimum(2*i+2,7),*A)
        return 0
    lax.fori_loop(0,4,step,0)
    for w in range(2):
        def pk(a,_):
            out_ref[w, :, pl.ds(pl.multiple_of(a*L,L),L)] = scr[w*128+a].astype(BF)
            return 0
        lax.fori_loop(0,128,pk,0,unroll=8)


def body(spectra, half_spectra, kernels, owners, counts, partners):
    x = spectra.reshape(2, 2, 33, 4, 128).transpose(0, 2, 3, 1, 4).reshape(2, 33, 8, 128)
    y = half_spectra.reshape(2, 2, 17, 4, 128).transpose(0, 2, 3, 1, 4).reshape(2, 17, 8, 128)
    k = kernels.reshape(16, 2, 4, 128).transpose(0, 2, 1, 3).reshape(128, 128)
    xc, yc = swapped(x), swapped(y)
    sent, rev = pl.pallas_call(
        pack_kernel,
        out_shape=(
            jax.ShapeDtypeStruct((64, 24, 128), BF),
            jax.ShapeDtypeStruct((128, 128), BF),
        ),
        in_specs=[SMEM] + [VMEM] * 6,
        out_specs=(VMEM, VMEM),
        name="pack",
    )(owners, partners.reshape(8, 128), k, x, y, xc, yc)
    got = lax.all_to_all(sent, TMPL, 0, 0, tiled=True)
    repeated, h = pl.pallas_call(
        relay_kernel,
        out_shape=(
            jax.ShapeDtypeStruct((64, 16, 128), BF),
            jax.ShapeDtypeStruct((16, 8, 128), BF),
        ),
        in_specs=[SMEM, SMEM, VMEM],
        out_specs=(VMEM, VMEM),
        name="relay",
    )(owners, partners, got)
    whole = lax.all_to_all(repeated, TMPL, 0, 0, tiled=True)
    out = pl.pallas_call(
        correlate_kernel,
        out_shape=jax.ShapeDtypeStruct((2, 16, 16384), BF),
        in_specs=[SMEM] + [VMEM] * 3,
        out_specs=VMEM,
        scratch_shapes=[
            pltpu.VMEM((2, 512, 128), F32),
            pltpu.VMEM((136, 128), F32),
            pltpu.VMEM((256, 1280), BF),
            pltpu.VMEM((256, 1280), BF),
            pltpu.VMEM((128, 128), F32),
            pltpu.VMEM((128, 128), F32),
            pltpu.VMEM((2, 1280, 256), BF),
            pltpu.VMEM((2, 1280, 256), BF),
            pltpu.VMEM((1280, 256), BF),
            pltpu.VMEM((1280, 256), BF),
            pltpu.VMEM((256, 16, 128), F32),
        ],
        name="correlate",
    )(counts, whole, rev, h.reshape(128, 128))
    return out[:, None]


def solution(mesh):
    finer = Mesh(
        mesh.devices.reshape(mesh.shape["trial"], 4, 4, 4), ("trial", "tmpl_0", "tmpl_1", "tmpl_2")
    )
    in_specs = (
        P(None, "trial", TMPL, None, None),
        P(None, "trial", TMPL, None, None),
        P(TMPL, None, None),
        P(),
        P(),
        P(),
    )
    out_specs = P(None, "trial", TMPL, None)
    return jax.shard_map(body, mesh=finer, in_specs=in_specs, out_specs=out_specs, check_vma=False)
```

```python
import jax
import jax.numpy as jnp
from jax import lax
from jax.experimental import pallas as pl
from jax.experimental.pallas import tpu as pltpu
from jax.sharding import Mesh
from jax.sharding import PartitionSpec as P

TMPL = ("tmpl_0", "tmpl_1", "tmpl_2")
F32 = jnp.float32
BF = jnp.bfloat16
L = 128
VMEM = pl.BlockSpec(memory_space=pltpu.VMEM)
SMEM = pl.BlockSpec(memory_space=pltpu.SMEM)
ANY = pl.BlockSpec(memory_space=pl.ANY)
SMALL = pltpu.CompilerParams(vmem_limit_bytes=4 << 20)
LARGE = pltpu.CompilerParams(vmem_limit_bytes=24 << 20)


def iota(shape, axis):
    return lax.broadcasted_iota(jnp.int32, shape, axis)


def dot(a, b):
    return jnp.dot(a, b, preferred_element_type=F32)


def pack_kernel(part_ref, k_ref, x_ref, y_ref, op_ref, buf, sems):
    me = lax.axis_index(TMPL)
    loads = []
    for w in range(2):
        rows = slice(8 + 8 * w, 16 + 8 * w)
        loads.append(pltpu.make_async_copy(x_ref.at[w], buf.at[0:33, rows, :], sems.at[2 * w]))
        loads.append(pltpu.make_async_copy(y_ref.at[w], buf.at[33:50, rows, :], sems.at[2 * w + 1]))
    for load in loads:
        load.start()
    buf[50:64, 8:24, :] = jnp.zeros((14, 16, L), BF)
    wanted = jnp.concatenate(
        [
            (jnp.broadcast_to(part_ref[r : r + 1, :], (L, L)) == me * 16 + iota((L, L), 0) // 8).astype(BF)
            for r in range(8)
        ],
        axis=0,
    )
    group = (iota((64, L), 0) // 8 == iota((64, L), 1) // 16).astype(BF)
    hit = lax.dot_general(group, wanted, (((1,), (1,)), ((), ())), preferred_element_type=F32)
    same = iota((64, L), 0) % 8 == iota((64, L), 1) % 8
    pick = jnp.concatenate(
        [jnp.where(same, hit[:, r * L : (r + 1) * L], 0.0).astype(BF) for r in range(8)], axis=0
    )
    buf[:, 0:8, :] = dot(pick, k_ref[...]).reshape(64, 8, L).astype(BF)
    for load in loads:
        load.wait()
    store = pltpu.make_async_copy(buf, op_ref, sems.at[4])
    store.start()
    store.wait()


def held_column(owners_ref, w, row):
    held = jnp.where(owners_ref[w, 0] // 64 == row, 0, 1)
    return owners_ref[w, held] % 64


def extract_kernel(owners_ref, got_ref, out_ref, sems):
    row = lax.axis_index("trial")
    copies = []
    for w in range(2):
        block = got_ref.at[held_column(owners_ref, w, row), 8 + 8 * w : 16 + 8 * w, :]
        copies.append(pltpu.make_async_copy(block, out_ref.at[w], sems.at[w]))
    for copy in copies:
        copy.start()
    for copy in copies:
        copy.wait()


def repeat_kernel(owners_ref, own_ref, other_ref, out_ref):
    for w in range(2):
        crossed = owners_ref[w, 0] >= 64
        block = jnp.where(crossed, other_ref[w].astype(F32), own_ref[w].astype(F32)).astype(BF)
        out_ref[:, 8 * w : 8 * w + 8, :] = jnp.broadcast_to(block[None], (64, 8, L))


def prepare_kernel(part_ref, k_ref, got_ref, rev_ref, h, sems):
    me = lax.axis_index(TMPL)
    copies = []
    for s in range(16):
        source = jnp.maximum(part_ref[me * 16 + s], 0) // 16
        copies.append(pltpu.make_async_copy(got_ref.at[source, 0:8, :], h.at[s], sems.at[s]))
    for copy in copies:
        copy.start()
    flip = (iota((L, L), 0) == (L - iota((L, L), 1)) % L).astype(BF)
    rev_ref[0] = dot(k_ref[...], flip)
    for copy in copies:
        copy.wait()
    rev_ref[1] = dot(h[...].astype(F32).reshape(L, L).astype(BF), flip)


def correlate_kernel(
    counts_ref, whole_ref, rev_ref, out_ref, whole, flat, y64, lx, ly, ra, rb, scr, obuf, sems
):
    me = lax.axis_index(TMPL)
    fetch = pltpu.make_async_copy(whole_ref, whole, sems.at[0])
    fetch.start()
    tri = iota((L, L), 0) >= iota((L, L), 1)
    tri_half = iota((L, L), 0) >= iota((L, L), 1) % 64
    left = iota((L, L), 1) < 64
    zero = jnp.zeros((L, L), F32)
    live_n = counts_ref[me]

    def circulant(kind, row, shift):
        v = jnp.broadcast_to(rev_ref[kind, pl.ds(row, 1), :], (L, L))
        return pltpu.roll(v, shift, 1, stride=1, stride_axis=0)

    def bands(cs, mask):
        first = [jnp.where(mask, cs[0], zero)]
        return first + [jnp.where(mask, cs[q], cs[q - 1]) for q in (1, 2, 3)] + [jnp.where(mask, zero, cs[3])]

    def put(dst, c, side, tiles):
        for q in range(5):
            dst[(5 * c + q) * L : (5 * c + q + 1) * L, side * L : (side + 1) * L] = tiles[q].astype(BF)

    def build(group, dst):
        for k in range(4):
            for c in range(2):
                row = (4 * group + k) * 8 + c
                put(dst.at[k // 2], c, k % 2, bands([circulant(0, row + 2 * q, 0) for q in range(4)], tri))
        for k in range(2):
            for c in range(2):
                row = (4 * group + 2 * k) * 8 + c
                both = [
                    jnp.where(left, circulant(1, row + 2 * q, 0), circulant(1, row + 8 + 2 * q, 64))
                    for q in range(4)
                ]
                put(dst.at[2], c, k, bands(both, tri_half))

    dup = (iota((L, 2 * L), 0) == (iota((L, 2 * L), 1) // L) * 64 + (iota((L, 2 * L), 1) % L) // 2).astype(BF)

    def power(rows, taps):
        z = dot(rows[...], taps[...])
        return z[:256] * z[:256] + z[256:] * z[256:]

    def work(group, src):
        plane = power(ly, src.at[2]).astype(BF)
        for k in range(2):
            wide = dot(plane[:, k * L : (k + 1) * L], dup)
            total = power(lx, src.at[k]) + wide
            for j in range(2):
                t = 4 * group + 2 * k + j
                scr[pl.ds(t, 256, stride=16), :] = jnp.where(t < live_n, total[:, j * L : (j + 1) * L], 0.0)

    build(0, ra)
    fetch.wait()
    lane = iota((68, L), 1)
    for w in range(2):
        flat[w] = whole[:, 8 * w : 8 * w + 8, :].astype(F32).reshape(512, L)
        top, low = slice(w * L, (w + 1) * L), slice(256 + w * L, 256 + (w + 1) * L)
        for c in range(2):
            even = flat[w, pl.ds(264 + c, 68, stride=2), :]
            after = flat[w, pl.ds(266 + c, 68, stride=2), :]
            y64[pl.ds(0, 68, stride=2), :] = even
            y64[pl.ds(1, 68, stride=2), :] = jnp.where(lane < 64, pltpu.roll(even, 64, 1), pltpu.roll(after, 64, 1))
            for q in range(5):
                here = slice((5 * c + q) * L, (5 * c + q + 1) * L)
                there = slice((5 - 5 * c + q) * L, (6 - 5 * c + q) * L)
                for dst, v in (
                    (lx, flat[w, pl.ds(2 * q + c, L, stride=2), :]),
                    (ly, y64[2 * q : 2 * q + L, :]),
                ):
                    dst[top, here] = (v if c == 0 else -v).astype(BF)
                    dst[low, there] = v.astype(BF)

    def step(i, carry):
        build(2 * i + 1, rb)
        work(2 * i, ra)
        build(jnp.minimum(2 * i + 2, 3), ra)
        work(2 * i + 1, rb)
        return carry

    lax.fori_loop(0, 2, step, 0)
    stores = []
    for w in range(2):

        def merge(a, carry):
            for u in range(8):
                at = (w * L + 8 * a + u) * 16
                cols = pl.ds(pl.multiple_of((8 * a + u) * L, L), L)
                obuf[w, :, cols] = scr[pl.ds(pl.multiple_of(at, 16), 16), :].astype(BF)
            return carry

        lax.fori_loop(0, 16, merge, 0)
        stores.append(pltpu.make_async_copy(obuf.at[w], out_ref.at[w], sems.at[1 + w]))
        stores[-1].start()
    for store in stores:
        store.wait()


def body(spectra, half_spectra, kernels, owners, counts, partners):
    x = spectra.reshape(2, 2, 33, 4, L).transpose(0, 2, 3, 1, 4).reshape(2, 33, 8, L)
    y = half_spectra.reshape(2, 2, 17, 4, L).transpose(0, 2, 3, 1, 4).reshape(2, 17, 8, L)
    k = kernels.reshape(16, 2, 4, L).transpose(0, 2, 1, 3).reshape(L, L)
    dma = pltpu.SemaphoreType.DMA
    sent = pl.pallas_call(
        pack_kernel,
        out_shape=jax.ShapeDtypeStruct((64, 24, L), BF),
        in_specs=[VMEM, VMEM, ANY, ANY],
        out_specs=ANY,
        scratch_shapes=[pltpu.VMEM((64, 24, L), BF), dma((5,))],
        name="pack",
    )(partners.reshape(8, L), k, x, y)
    got = lax.all_to_all(sent, TMPL, 0, 0, tiled=True)
    own = pl.pallas_call(
        extract_kernel,
        out_shape=jax.ShapeDtypeStruct((2, 8, L), BF),
        in_specs=[SMEM, ANY],
        out_specs=VMEM,
        scratch_shapes=[dma((2,))],
        compiler_params=SMALL,
        name="extract",
    )(owners, got)
    other = lax.ppermute(own, "trial", [(0, 1), (1, 0)])
    repeated = pl.pallas_call(
        repeat_kernel,
        out_shape=jax.ShapeDtypeStruct((64, 16, L), BF),
        in_specs=[SMEM, VMEM, VMEM],
        out_specs=VMEM,
        compiler_params=SMALL,
        name="repeat",
    )(owners, own, other)
    rev = pl.pallas_call(
        prepare_kernel,
        out_shape=jax.ShapeDtypeStruct((2, L, L), F32),
        in_specs=[SMEM, VMEM, ANY],
        out_specs=VMEM,
        scratch_shapes=[pltpu.VMEM((16, 8, L), BF), dma((16,))],
        cost_estimate=pl.CostEstimate(flops=10**7, bytes_accessed=10**6, transcendentals=0),
        compiler_params=SMALL,
        name="prepare",
    )(partners, k, got)
    whole = lax.all_to_all(repeated, TMPL, 0, 0, tiled=True)
    out = pl.pallas_call(
        correlate_kernel,
        out_shape=jax.ShapeDtypeStruct((2, 16, 16384), BF),
        in_specs=[SMEM, ANY, VMEM],
        out_specs=ANY,
        scratch_shapes=[
            pltpu.VMEM((64, 16, L), BF),
            pltpu.VMEM((2, 512, L), F32),
            pltpu.VMEM((136, L), F32),
            pltpu.VMEM((512, 1280), BF),
            pltpu.VMEM((512, 1280), BF),
            pltpu.VMEM((3, 1280, 256), BF),
            pltpu.VMEM((3, 1280, 256), BF),
            pltpu.VMEM((4096, L), F32),
            pltpu.VMEM((2, 16, 16384), BF),
            dma((3,)),
        ],
        compiler_params=LARGE,
        name="correlate",
    )(counts, whole, rev)
    return out[:, None]


def solution(mesh):
    finer = Mesh(
        mesh.devices.reshape(mesh.shape["trial"], 4, 4, 4), ("trial", "tmpl_0", "tmpl_1", "tmpl_2")
    )
    in_specs = (
        P(None, "trial", TMPL, None, None),
        P(None, "trial", TMPL, None, None),
        P(TMPL, None, None),
        P(),
        P(),
        P(),
    )
    out_specs = P(None, "trial", TMPL, None)
    return jax.shard_map(body, mesh=finer, in_specs=in_specs, out_specs=out_specs, check_vma=False)
```

```python
import jax
import jax.numpy as jnp
from jax import lax
from jax.experimental import pallas as pl
from jax.experimental.pallas import tpu as pltpu
from jax.sharding import Mesh
from jax.sharding import PartitionSpec as P

TMPL = ("tmpl_0", "tmpl_1", "tmpl_2")
F32 = jnp.float32
BF = jnp.bfloat16
L = 128
VMEM = pl.BlockSpec(memory_space=pltpu.VMEM)
SMEM = pl.BlockSpec(memory_space=pltpu.SMEM)
ANY = pl.BlockSpec(memory_space=pl.ANY)
SMALL = pltpu.CompilerParams(vmem_limit_bytes=4 << 20)
LARGE = pltpu.CompilerParams(vmem_limit_bytes=24 << 20)


def iota(shape, axis):
    return lax.broadcasted_iota(jnp.int32, shape, axis)


def dot(a, b):
    return jnp.dot(a, b, preferred_element_type=F32)


def pack_kernel(part_ref, k_ref, x_ref, y_ref, op_ref, buf, sems):
    me = lax.axis_index(TMPL)
    loads = []
    for w in range(2):
        rows = slice(8 + 8 * w, 16 + 8 * w)
        loads.append(pltpu.make_async_copy(x_ref.at[w], buf.at[0:33, rows, :], sems.at[2 * w]))
        loads.append(pltpu.make_async_copy(y_ref.at[w], buf.at[33:50, rows, :], sems.at[2 * w + 1]))
    for load in loads:
        load.start()
    buf[50:64, 8:24, :] = jnp.zeros((14, 16, L), BF)
    wanted = jnp.concatenate(
        [
            (jnp.broadcast_to(part_ref[r : r + 1, :], (L, L)) == me * 16 + iota((L, L), 0) // 8).astype(BF)
            for r in range(8)
        ],
        axis=0,
    )
    group = (iota((64, L), 0) // 8 == iota((64, L), 1) // 16).astype(BF)
    hit = lax.dot_general(group, wanted, (((1,), (1,)), ((), ())), preferred_element_type=F32)
    same = iota((64, L), 0) % 8 == iota((64, L), 1) % 8
    pick = jnp.concatenate(
        [jnp.where(same, hit[:, r * L : (r + 1) * L], 0.0).astype(BF) for r in range(8)], axis=0
    )
    buf[:, 0:8, :] = dot(pick, k_ref[...]).reshape(64, 8, L).astype(BF)
    for load in loads:
        load.wait()
    store = pltpu.make_async_copy(buf, op_ref, sems.at[4])
    store.start()
    store.wait()


def held_column(owners_ref, w, row):
    held = jnp.where(owners_ref[w, 0] // 64 == row, 0, 1)
    return owners_ref[w, held] % 64


def extract_kernel(owners_ref, got_ref, out_ref, sems):
    row = lax.axis_index("trial")
    copies = []
    for w in range(2):
        block = got_ref.at[held_column(owners_ref, w, row), 8 + 8 * w : 16 + 8 * w, :]
        copies.append(pltpu.make_async_copy(block, out_ref.at[w], sems.at[w]))
    for copy in copies:
        copy.start()
    for copy in copies:
        copy.wait()


def repeat_kernel(owners_ref, own_ref, other_ref, out_ref):
    for w in range(2):
        crossed = owners_ref[w, 0] >= 64
        block = jnp.where(crossed, other_ref[w].astype(F32), own_ref[w].astype(F32)).astype(BF)
        out_ref[:, 8 * w : 8 * w + 8, :] = jnp.broadcast_to(block[None], (64, 8, L))


def prepare_kernel(part_ref, k_ref, got_ref, rev_ref, h, sems):
    me = lax.axis_index(TMPL)
    copies = []
    for s in range(16):
        source = jnp.maximum(part_ref[me * 16 + s], 0) // 16
        copies.append(pltpu.make_async_copy(got_ref.at[source, 0:8, :], h.at[s], sems.at[s]))
    for copy in copies:
        copy.start()
    flip = (iota((L, L), 0) == (L - iota((L, L), 1)) % L).astype(BF)
    rev_ref[0] = dot(k_ref[...], flip)
    for copy in copies:
        copy.wait()
    rev_ref[1] = dot(h[...].astype(F32).reshape(L, L).astype(BF), flip)


def correlate_kernel(
    counts_ref, whole, rev_ref, out_ref, flat, y64, lx, ly, ra, rb, scr, obuf, sems
):
    me = lax.axis_index(TMPL)
    tri = iota((L, L), 0) >= iota((L, L), 1)
    tri_half = iota((L, L), 0) >= iota((L, L), 1) % 64
    left = iota((L, L), 1) < 64
    zero = jnp.zeros((L, L), F32)
    live_n = counts_ref[me]

    def circulant(kind, row, shift):
        v = jnp.broadcast_to(rev_ref[kind, pl.ds(row, 1), :], (L, L))
        return pltpu.roll(v, shift, 1, stride=1, stride_axis=0)

    def bands(cs, mask):
        first = [jnp.where(mask, cs[0], zero)]
        return first + [jnp.where(mask, cs[q], cs[q - 1]) for q in (1, 2, 3)] + [jnp.where(mask, zero, cs[3])]

    def put(dst, c, side, tiles):
        for q in range(5):
            dst[(5 * c + q) * L : (5 * c + q + 1) * L, side * L : (side + 1) * L] = tiles[q].astype(BF)

    def build(group, dst):
        for k in range(4):
            for c in range(2):
                row = (4 * group + k) * 8 + c
                put(dst.at[k // 2], c, k % 2, bands([circulant(0, row + 2 * q, 0) for q in range(4)], tri))
        for k in range(2):
            for c in range(2):
                row = (4 * group + 2 * k) * 8 + c
                both = [
                    jnp.where(left, circulant(1, row + 2 * q, 0), circulant(1, row + 8 + 2 * q, 64))
                    for q in range(4)
                ]
                put(dst.at[2], c, k, bands(both, tri_half))

    dup = (iota((L, 2 * L), 0) == (iota((L, 2 * L), 1) // L) * 64 + (iota((L, 2 * L), 1) % L) // 2).astype(BF)

    def power(rows, taps):
        re = dot(rows[0:256, :], taps[...])
        im = dot(rows[256:512, :], taps[...])
        return re * re + im * im

    def work(group, src):
        plane = power(ly, src.at[2]).astype(BF)
        for k in range(2):
            wide = dot(plane[:, k * L : (k + 1) * L], dup)
            total = power(lx, src.at[k]) + wide
            for j in range(2):
                t = 4 * group + 2 * k + j
                scr[pl.ds(t, 256, stride=16), :] = jnp.where(t < live_n, total[:, j * L : (j + 1) * L], 0.0)

    build(0, ra)
    lane = iota((68, L), 1)
    for w in range(2):
        flat[w] = whole[:, 8 * w : 8 * w + 8, :].astype(F32).reshape(512, L)
        top, low = slice(w * L, (w + 1) * L), slice(256 + w * L, 256 + (w + 1) * L)
        for c in range(2):
            even = flat[w, pl.ds(264 + c, 68, stride=2), :]
            after = flat[w, pl.ds(266 + c, 68, stride=2), :]
            y64[pl.ds(0, 68, stride=2), :] = even
            y64[pl.ds(1, 68, stride=2), :] = jnp.where(lane < 64, pltpu.roll(even, 64, 1), pltpu.roll(after, 64, 1))
            for q in range(5):
                here = slice((5 * c + q) * L, (5 * c + q + 1) * L)
                there = slice((5 - 5 * c + q) * L, (6 - 5 * c + q) * L)
                for dst, v in (
                    (lx, flat[w, pl.ds(2 * q + c, L, stride=2), :]),
                    (ly, y64[2 * q : 2 * q + L, :]),
                ):
                    dst[top, here] = (v if c == 0 else -v).astype(BF)
                    dst[low, there] = v.astype(BF)

    for group in range(4):
        if group < 3:
            build(group + 1, (ra, rb)[(group + 1) % 2])
        work(group, (ra, rb)[group % 2])
    stores = []
    for part in range(8):
        w, first = part // 4, part % 4 * 32

        def merge(a, carry):
            for u in range(8):
                at = first + 8 * a + u
                cols = pl.ds(pl.multiple_of(at * L, L), L)
                rows = pl.ds(pl.multiple_of((w * L + at) * 16, 16), 16)
                obuf[w, :, cols] = scr[rows, :].astype(BF)
            return carry

        lax.fori_loop(0, 4, merge, 0, unroll=True)
        cols = slice(first * L, (first + 32) * L)
        stores.append(pltpu.make_async_copy(obuf.at[w, :, cols], out_ref.at[w, :, cols], sems.at[part]))
        stores[-1].start()
    for store in stores:
        store.wait()


def body(spectra, half_spectra, kernels, owners, counts, partners):
    x = spectra.reshape(2, 2, 33, 4, L).transpose(0, 2, 3, 1, 4).reshape(2, 33, 8, L)
    y = half_spectra.reshape(2, 2, 17, 4, L).transpose(0, 2, 3, 1, 4).reshape(2, 17, 8, L)
    k = kernels.reshape(16, 2, 4, L).transpose(0, 2, 1, 3).reshape(L, L)
    dma = pltpu.SemaphoreType.DMA
    sent = pl.pallas_call(
        pack_kernel,
        out_shape=jax.ShapeDtypeStruct((64, 24, L), BF),
        in_specs=[VMEM, VMEM, ANY, ANY],
        out_specs=ANY,
        scratch_shapes=[pltpu.VMEM((64, 24, L), BF), dma((5,))],
        name="pack",
    )(partners.reshape(8, L), k, x, y)
    got = lax.all_to_all(sent, TMPL, 0, 0, tiled=True)
    own = pl.pallas_call(
        extract_kernel,
        out_shape=jax.ShapeDtypeStruct((2, 8, L), BF),
        in_specs=[SMEM, ANY],
        out_specs=VMEM,
        scratch_shapes=[dma((2,))],
        compiler_params=SMALL,
        name="extract",
    )(owners, got)
    other = lax.ppermute(own, "trial", [(0, 1), (1, 0)])
    repeated = pl.pallas_call(
        repeat_kernel,
        out_shape=jax.ShapeDtypeStruct((64, 16, L), BF),
        in_specs=[SMEM, VMEM, VMEM],
        out_specs=VMEM,
        compiler_params=SMALL,
        name="repeat",
    )(owners, own, other)
    rev = pl.pallas_call(
        prepare_kernel,
        out_shape=jax.ShapeDtypeStruct((2, L, L), F32),
        in_specs=[SMEM, VMEM, ANY],
        out_specs=VMEM,
        scratch_shapes=[pltpu.VMEM((16, 8, L), BF), dma((16,))],
        cost_estimate=pl.CostEstimate(flops=10**7, bytes_accessed=10**6, transcendentals=0),
        compiler_params=SMALL,
        name="prepare",
    )(partners, k, got)
    whole = lax.all_to_all(repeated, TMPL, 0, 0, tiled=True)
    out = pl.pallas_call(
        correlate_kernel,
        out_shape=jax.ShapeDtypeStruct((2, 16, 16384), BF),
        in_specs=[SMEM, VMEM, VMEM],
        out_specs=ANY,
        scratch_shapes=[
            pltpu.VMEM((2, 512, L), F32),
            pltpu.VMEM((136, L), F32),
            pltpu.VMEM((512, 1280), BF),
            pltpu.VMEM((512, 1280), BF),
            pltpu.VMEM((3, 1280, 256), BF),
            pltpu.VMEM((3, 1280, 256), BF),
            pltpu.VMEM((4096, L), F32),
            pltpu.VMEM((2, 16, 16384), BF),
            dma((8,)),
        ],
        compiler_params=LARGE,
        name="correlate",
    )(counts, whole, rev)
    return out[:, None]


def solution(mesh):
    finer = Mesh(
        mesh.devices.reshape(mesh.shape["trial"], 4, 4, 4), ("trial", "tmpl_0", "tmpl_1", "tmpl_2")
    )
    in_specs = (
        P(None, "trial", TMPL, None, None),
        P(None, "trial", TMPL, None, None),
        P(TMPL, None, None),
        P(),
        P(),
        P(),
    )
    out_specs = P(None, "trial", TMPL, None)
    return jax.shard_map(body, mesh=finer, in_specs=in_specs, out_specs=out_specs, check_vma=False)
```

```python
import jax
import jax.numpy as jnp
from jax import lax
from jax.experimental import pallas as pl
from jax.experimental.pallas import tpu as pltpu
from jax.sharding import Mesh
from jax.sharding import PartitionSpec as P

TMPL = ("tmpl_0", "tmpl_1", "tmpl_2")
F32 = jnp.float32
BF = jnp.bfloat16
L = 128
VMEM = pl.BlockSpec(memory_space=pltpu.VMEM)
SMEM = pl.BlockSpec(memory_space=pltpu.SMEM)
ANY = pl.BlockSpec(memory_space=pl.ANY)
SMALL = pltpu.CompilerParams(vmem_limit_bytes=4 << 20)
LARGE = pltpu.CompilerParams(vmem_limit_bytes=24 << 20)


def iota(shape, axis):
    return lax.broadcasted_iota(jnp.int32, shape, axis)


def dot(a, b):
    return jnp.dot(a, b, preferred_element_type=F32)


def pack_kernel(part_hbm, k_hbm, x_ref, y_ref, op_ref, part_ref, k_ref, buf, sems):
    me = lax.axis_index(TMPL)
    tables = (
        pltpu.make_async_copy(part_hbm, part_ref, sems.at[5]),
        pltpu.make_async_copy(k_hbm, k_ref, sems.at[6]),
    )
    for table in tables:
        table.start()
    loads = []
    for w in range(2):
        rows = slice(8 + 8 * w, 16 + 8 * w)
        loads.append(pltpu.make_async_copy(x_ref.at[w], buf.at[0:33, rows, :], sems.at[2 * w]))
        loads.append(pltpu.make_async_copy(y_ref.at[w], buf.at[33:50, rows, :], sems.at[2 * w + 1]))
    for load in loads:
        load.start()
    buf[50:64, 8:24, :] = jnp.zeros((14, 16, L), BF)
    group = (iota((64, L), 0) // 8 == iota((64, L), 1) // 16).astype(BF)
    same = iota((64, L), 0) % 8 == iota((64, L), 1) % 8
    for table in tables:
        table.wait()
    wanted = jnp.concatenate(
        [
            (jnp.broadcast_to(part_ref[r : r + 1, :], (L, L)) == me * 16 + iota((L, L), 0) // 8).astype(BF)
            for r in range(8)
        ],
        axis=0,
    )
    hit = lax.dot_general(group, wanted, (((1,), (1,)), ((), ())), preferred_element_type=F32)
    pick = jnp.concatenate(
        [jnp.where(same, hit[:, r * L : (r + 1) * L], 0.0).astype(BF) for r in range(8)], axis=0
    )
    buf[:, 0:8, :] = dot(pick, k_ref[...]).reshape(64, 8, L).astype(BF)
    for load in loads:
        load.wait()
    store = pltpu.make_async_copy(buf, op_ref, sems.at[4])
    store.start()
    store.wait()


def relay_kernel(owners_ref, got_ref, out_ref):
    row = lax.axis_index("trial")
    for dest in range(2):
        w = jnp.where(owners_ref[0, dest] // 64 == row, 0, 1)
        start = pl.multiple_of(8 + 8 * w, 8)
        block = got_ref[owners_ref[w, dest] % 64, pl.ds(start, 8), :]
        out_ref[64 * dest : 64 * dest + 64] = jnp.broadcast_to(block[None], (64, 8, L))


def prepare_kernel(part_ref, k_ref, got_ref, rev_ref, h, sems):
    me = lax.axis_index(TMPL)
    copies = []
    for s in range(16):
        source = jnp.maximum(part_ref[me * 16 + s], 0) // 16
        copies.append(pltpu.make_async_copy(got_ref.at[source, 0:8, :], h.at[s], sems.at[s]))
    for copy in copies:
        copy.start()
    flip = (iota((L, L), 0) == (L - iota((L, L), 1)) % L).astype(BF)
    rev_ref[0] = dot(k_ref[...], flip)
    for copy in copies:
        copy.wait()
    rev_ref[1] = dot(h[...].astype(F32).reshape(L, L).astype(BF), flip)


def correlate_kernel(
    counts_ref, owners_ref, whole, rev_ref, out_ref, flat, y64, lx, ly, ra, rb, scr, obuf, sems
):
    me = lax.axis_index(TMPL)
    tri = iota((L, L), 0) >= iota((L, L), 1)
    tri_half = iota((L, L), 0) >= iota((L, L), 1) % 64
    left = iota((L, L), 1) < 64
    zero = jnp.zeros((L, L), F32)
    live_n = counts_ref[me]

    def circulant(kind, row, shift):
        v = jnp.broadcast_to(rev_ref[kind, pl.ds(row, 1), :], (L, L))
        return pltpu.roll(v, shift, 1, stride=1, stride_axis=0)

    def bands(cs, mask):
        first = [jnp.where(mask, cs[0], zero)]
        return first + [jnp.where(mask, cs[q], cs[q - 1]) for q in (1, 2, 3)] + [jnp.where(mask, zero, cs[3])]

    def put(dst, c, side, tiles):
        for q in range(5):
            dst[(5 * c + q) * L : (5 * c + q + 1) * L, side * L : (side + 1) * L] = tiles[q].astype(BF)

    def build(group, dst):
        for k in range(4):
            for c in range(2):
                row = (4 * group + k) * 8 + c
                put(dst.at[k // 2], c, k % 2, bands([circulant(0, row + 2 * q, 0) for q in range(4)], tri))
        for k in range(2):
            for c in range(2):
                row = (4 * group + 2 * k) * 8 + c
                both = [
                    jnp.where(left, circulant(1, row + 2 * q, 0), circulant(1, row + 8 + 2 * q, 64))
                    for q in range(4)
                ]
                put(dst.at[2], c, k, bands(both, tri_half))

    dup = (iota((L, 2 * L), 0) == (iota((L, 2 * L), 1) // L) * 64 + (iota((L, 2 * L), 1) % L) // 2).astype(BF)

    def power(rows, taps):
        re = dot(rows[0:256, :], taps[...])
        im = dot(rows[256:512, :], taps[...])
        return re * re + im * im

    def work(group, src):
        plane = power(ly, src.at[2]).astype(BF)
        for k in range(2):
            wide = dot(plane[:, k * L : (k + 1) * L], dup)
            total = power(lx, src.at[k]) + wide
            for j in range(2):
                t = 4 * group + 2 * k + j
                scr[pl.ds(t, 256, stride=16), :] = jnp.where(t < live_n, total[:, j * L : (j + 1) * L], 0.0)

    build(0, ra)
    lane = iota((68, L), 1)
    for w in range(2):
        held = owners_ref[w, lax.axis_index("trial")] // 64
        flat[w] = whole[pl.ds(64 * held, 64)].astype(F32).reshape(512, L)
        top, low = slice(w * L, (w + 1) * L), slice(256 + w * L, 256 + (w + 1) * L)
        for c in range(2):
            even = flat[w, pl.ds(264 + c, 68, stride=2), :]
            after = flat[w, pl.ds(266 + c, 68, stride=2), :]
            y64[pl.ds(0, 68, stride=2), :] = even
            y64[pl.ds(1, 68, stride=2), :] = jnp.where(lane < 64, pltpu.roll(even, 64, 1), pltpu.roll(after, 64, 1))
            for q in range(5):
                here = slice((5 * c + q) * L, (5 * c + q + 1) * L)
                there = slice((5 - 5 * c + q) * L, (6 - 5 * c + q) * L)
                for dst, v in (
                    (lx, flat[w, pl.ds(2 * q + c, L, stride=2), :]),
                    (ly, y64[2 * q : 2 * q + L, :]),
                ):
                    dst[top, here] = (v if c == 0 else -v).astype(BF)
                    dst[low, there] = v.astype(BF)

    for group in range(4):
        if group < 3:
            build(group + 1, (ra, rb)[(group + 1) % 2])
        work(group, (ra, rb)[group % 2])
    stores = []
    for part in range(8):
        w, first = part // 4, part % 4 * 32

        def merge(a, carry):
            for u in range(8):
                at = first + 8 * a + u
                cols = pl.ds(pl.multiple_of(at * L, L), L)
                rows = pl.ds(pl.multiple_of((w * L + at) * 16, 16), 16)
                obuf[w, :, cols] = scr[rows, :].astype(BF)
            return carry

        lax.fori_loop(0, 4, merge, 0, unroll=True)
        cols = slice(first * L, (first + 32) * L)
        stores.append(pltpu.make_async_copy(obuf.at[w, :, cols], out_ref.at[w, :, cols], sems.at[part]))
        stores[-1].start()
    for store in stores:
        store.wait()


def body(spectra, half_spectra, kernels, owners, counts, partners):
    x = spectra.reshape(2, 2, 33, 4, L).transpose(0, 2, 3, 1, 4).reshape(2, 33, 8, L)
    y = half_spectra.reshape(2, 2, 17, 4, L).transpose(0, 2, 3, 1, 4).reshape(2, 17, 8, L)
    k = kernels.reshape(16, 2, 4, L).transpose(0, 2, 1, 3).reshape(L, L)
    dma = pltpu.SemaphoreType.DMA
    sent = pl.pallas_call(
        pack_kernel,
        out_shape=jax.ShapeDtypeStruct((64, 24, L), BF),
        in_specs=[ANY] * 4,
        out_specs=ANY,
        scratch_shapes=[
            pltpu.VMEM((8, L), jnp.int32),
            pltpu.VMEM((L, L), BF),
            pltpu.VMEM((64, 24, L), BF),
            dma((7,)),
        ],
        name="pack",
    )(partners.reshape(8, L), k, x, y)
    got = lax.all_to_all(sent, TMPL, 0, 0, tiled=True)
    repeated = pl.pallas_call(
        relay_kernel,
        out_shape=jax.ShapeDtypeStruct((128, 8, L), BF),
        in_specs=[SMEM, VMEM],
        out_specs=VMEM,
        compiler_params=SMALL,
        name="relay",
    )(owners, got)
    rev = pl.pallas_call(
        prepare_kernel,
        out_shape=jax.ShapeDtypeStruct((2, L, L), F32),
        in_specs=[SMEM, VMEM, ANY],
        out_specs=VMEM,
        scratch_shapes=[pltpu.VMEM((16, 8, L), BF), dma((16,))],
        cost_estimate=pl.CostEstimate(flops=10**7, bytes_accessed=10**6, transcendentals=0),
        compiler_params=SMALL,
        name="prepare",
    )(partners, k, got)
    whole = lax.all_to_all(repeated, ("trial",) + TMPL, 0, 0, tiled=True)
    out = pl.pallas_call(
        correlate_kernel,
        out_shape=jax.ShapeDtypeStruct((2, 16, 16384), BF),
        in_specs=[SMEM, SMEM, VMEM, VMEM],
        out_specs=ANY,
        scratch_shapes=[
            pltpu.VMEM((2, 512, L), F32),
            pltpu.VMEM((136, L), F32),
            pltpu.VMEM((512, 1280), BF),
            pltpu.VMEM((512, 1280), BF),
            pltpu.VMEM((3, 1280, 256), BF),
            pltpu.VMEM((3, 1280, 256), BF),
            pltpu.VMEM((4096, L), F32),
            pltpu.VMEM((2, 16, 16384), BF),
            dma((8,)),
        ],
        compiler_params=LARGE,
        name="correlate",
    )(counts, owners, whole, rev)
    return out[:, None]


def solution(mesh):
    finer = Mesh(
        mesh.devices.reshape(mesh.shape["trial"], 4, 4, 4), ("trial", "tmpl_0", "tmpl_1", "tmpl_2")
    )
    in_specs = (
        P(None, "trial", TMPL, None, None),
        P(None, "trial", TMPL, None, None),
        P(TMPL, None, None),
        P(),
        P(),
        P(),
    )
    out_specs = P(None, "trial", TMPL, None)
    return jax.shard_map(body, mesh=finer, in_specs=in_specs, out_specs=out_specs, check_vma=False)
```

```python
import jax
import jax.numpy as jnp
from jax import lax
from jax.experimental import pallas as pl
from jax.experimental.pallas import tpu as pltpu
from jax.sharding import Mesh
from jax.sharding import PartitionSpec as P

TMPL = ("tmpl_0", "tmpl_1", "tmpl_2")
F32 = jnp.float32
BF = jnp.bfloat16
L = 128
VMEM = pl.BlockSpec(memory_space=pltpu.VMEM)
SMEM = pl.BlockSpec(memory_space=pltpu.SMEM)
ANY = pl.BlockSpec(memory_space=pl.ANY)
SMALL = pltpu.CompilerParams(vmem_limit_bytes=4 << 20)
LARGE = pltpu.CompilerParams(vmem_limit_bytes=24 << 20)


def iota(shape, axis):
    return lax.broadcasted_iota(jnp.int32, shape, axis)


def dot(a, b):
    return jnp.dot(a, b, preferred_element_type=F32)


def pack_kernel(part_hbm, k_hbm, x_ref, y_ref, buf, part_ref, k_ref, sems):
    me = lax.axis_index(TMPL)
    tables = (
        pltpu.make_async_copy(part_hbm, part_ref, sems.at[4]),
        pltpu.make_async_copy(k_hbm, k_ref, sems.at[5]),
    )
    for table in tables:
        table.start()
    loads = []
    for w in range(2):
        rows = slice(8 + 8 * w, 16 + 8 * w)
        loads.append(pltpu.make_async_copy(x_ref.at[w], buf.at[0:33, rows, :], sems.at[2 * w]))
        loads.append(pltpu.make_async_copy(y_ref.at[w], buf.at[33:50, rows, :], sems.at[2 * w + 1]))
    for load in loads:
        load.start()
    buf[50:64, 8:24, :] = jnp.zeros((14, 16, L), BF)
    group = (iota((64, L), 0) // 8 == iota((64, L), 1) // 16).astype(BF)
    same = iota((64, L), 0) % 8 == iota((64, L), 1) % 8
    for table in tables:
        table.wait()
    wanted = jnp.concatenate(
        [
            (jnp.broadcast_to(part_ref[r : r + 1, :], (L, L)) == me * 16 + iota((L, L), 0) // 8).astype(BF)
            for r in range(8)
        ],
        axis=0,
    )
    hit = lax.dot_general(group, wanted, (((1,), (1,)), ((), ())), preferred_element_type=F32)
    pick = jnp.concatenate(
        [jnp.where(same, hit[:, r * L : (r + 1) * L], 0.0).astype(BF) for r in range(8)], axis=0
    )
    buf[:, 0:8, :] = dot(pick, k_ref[...]).reshape(64, 8, L).astype(BF)
    for load in loads:
        load.wait()


def relay_kernel(owners_ref, got_ref, out_ref):
    row = lax.axis_index("trial")
    for dest in range(2):
        w = jnp.where(owners_ref[0, dest] // 64 == row, 0, 1)
        start = pl.multiple_of(8 + 8 * w, 8)
        block = got_ref[owners_ref[w, dest] % 64, pl.ds(start, 8), :]
        out_ref[64 * dest : 64 * dest + 64] = jnp.broadcast_to(block[None], (64, 8, L))


class Taps:
    def __init__(self, rev_ref):
        self.rev = rev_ref
        self.tri = iota((L, L), 0) >= iota((L, L), 1)
        self.tri_half = iota((L, L), 0) >= iota((L, L), 1) % 64
        self.left = iota((L, L), 1) < 64
        self.zero = jnp.zeros((L, L), F32)

    def circulant(self, kind, row, shift):
        v = jnp.broadcast_to(self.rev[kind, pl.ds(row, 1), :], (L, L))
        return pltpu.roll(v, shift, 1, stride=1, stride_axis=0)

    def put(self, dst, c, side, cs, mask):
        lower = cs + [self.zero]
        upper = [self.zero] + cs
        for q in range(5):
            tile = jnp.where(mask, lower[q], upper[q]).astype(BF)
            dst[(5 * c + q) * L : (5 * c + q + 1) * L, side * L : (side + 1) * L] = tile

    def direct(self, pair, dst):
        for k in range(2):
            for c in range(2):
                row = (2 * pair + k) * 8 + c
                self.put(dst, c, k, [self.circulant(0, row + 2 * q, 0) for q in range(4)], self.tri)

    def plane(self, group, dst):
        for k in range(2):
            for c in range(2):
                row = (4 * group + 2 * k) * 8 + c
                both = [
                    jnp.where(self.left, self.circulant(1, row + 2 * q, 0), self.circulant(1, row + 8 + 2 * q, 64))
                    for q in range(4)
                ]
                self.put(dst, c, k, both, self.tri_half)


def prepare_kernel(part_ref, k_ref, got_ref, rev_ref, ahead_ref, h, sems):
    me = lax.axis_index(TMPL)
    copies = []
    for s in range(16):
        source = jnp.maximum(part_ref[me * 16 + s], 0) // 16
        copies.append(pltpu.make_async_copy(got_ref.at[source, 0:8, :], h.at[s], sems.at[s]))
    for copy in copies:
        copy.start()
    flip = (iota((L, L), 0) == (L - iota((L, L), 1)) % L).astype(BF)
    rev_ref[0] = dot(k_ref[...], flip)
    for copy in copies:
        copy.wait()
    rev_ref[1] = dot(h[...].astype(F32).reshape(L, L).astype(BF), flip)
    taps = Taps(rev_ref)
    for group in range(2):
        taps.plane(group, ahead_ref.at[group])


def correlate_kernel(
    counts_ref, owners_ref, whole, rev_ref, ahead, out_ref, flat, y64, lx, ly, rp, rd, scr, obuf, sems
):
    me = lax.axis_index(TMPL)
    live_n = counts_ref[me]
    taps = Taps(rev_ref)

    dup = (iota((L, 2 * L), 0) == (iota((L, 2 * L), 1) // L) * 64 + (iota((L, 2 * L), 1) % L) // 2).astype(BF)

    def power(rows, w, operand):
        z = dot(rows[256 * w : 256 * w + 256, :], operand[...])
        return z[:L] * z[:L] + z[L:] * z[L:]

    def finish(pair, w, plane):
        wide = dot(plane[:, (pair % 2) * L : (pair % 2 + 1) * L], dup)
        total = power(lx, w, rd.at[pair]) + wide
        for j in range(2):
            t = 2 * pair + j
            rows = pl.ds(w * 2048 + t, L, stride=16)
            scr[rows, :] = jnp.where(t < live_n, total[:, j * L : (j + 1) * L], 0.0)

    stores = []

    def merge(w):
        for part in range(4):
            for a in range(32 * part, 32 * part + 32):
                rows = slice((w * L + a) * 16, (w * L + a + 1) * 16)
                obuf[w, :, a * L : (a + 1) * L] = scr[rows, :].astype(BF)
            cols = slice(part * 4096, (part + 1) * 4096)
            copy = pltpu.make_async_copy(obuf.at[w, :, cols], out_ref.at[w, :, cols], sems.at[4 * w + part])
            copy.start()
            stores.append(copy)

    lane = iota((68, L), 1)
    for w in range(2):
        held = owners_ref[w, lax.axis_index("trial")] // 64
        flat[w] = whole[pl.ds(64 * held, 64)].astype(F32).reshape(512, L)
        top, low = slice(256 * w, 256 * w + L), slice(256 * w + L, 256 * w + 256)
        for c in range(2):
            even = flat[w, pl.ds(264 + c, 68, stride=2), :]
            after = flat[w, pl.ds(266 + c, 68, stride=2), :]
            y64[pl.ds(0, 68, stride=2), :] = even
            y64[pl.ds(1, 68, stride=2), :] = jnp.where(lane < 64, pltpu.roll(even, 64, 1), pltpu.roll(after, 64, 1))
            for q in range(5):
                here = slice((5 * c + q) * L, (5 * c + q + 1) * L)
                there = slice((5 - 5 * c + q) * L, (6 - 5 * c + q) * L)
                for dst, v in (
                    (lx, flat[w, pl.ds(2 * q + c, L, stride=2), :]),
                    (ly, y64[2 * q : 2 * q + L, :]),
                ):
                    dst[top, here] = (v if c == 0 else -v).astype(BF)
                    dst[low, there] = v.astype(BF)

    for half in range(2):
        pairs = range(4 * half, 4 * half + 4)
        taps.direct(pairs[0], rd.at[pairs[0]])
        taps.direct(pairs[1], rd.at[pairs[1]])
        planes = [[power(ly, w, (rp if half else ahead).at[k]).astype(BF) for w in range(2)] for k in range(2)]
        taps.direct(pairs[2], rd.at[pairs[2]])
        taps.direct(pairs[3], rd.at[pairs[3]])
        if half == 0:
            for pair in pairs:
                if pair == 2:
                    taps.plane(2, rp.at[0])
                    taps.plane(3, rp.at[1])
                for w in range(2):
                    finish(pair, w, planes[pair // 2 % 2][w])
        else:
            for w in range(2):
                for pair in pairs:
                    finish(pair, w, planes[pair // 2 % 2][w])
                merge(w)
    for store in stores:
        store.wait()


def body(spectra, half_spectra, kernels, owners, counts, partners):
    x = spectra.reshape(2, 2, 33, 4, L).transpose(0, 2, 3, 1, 4).reshape(2, 33, 8, L)
    y = half_spectra.reshape(2, 2, 17, 4, L).transpose(0, 2, 3, 1, 4).reshape(2, 17, 8, L)
    k = kernels.reshape(16, 2, 4, L).transpose(0, 2, 1, 3).reshape(L, L)
    dma = pltpu.SemaphoreType.DMA
    sent = pl.pallas_call(
        pack_kernel,
        out_shape=jax.ShapeDtypeStruct((64, 24, L), BF),
        in_specs=[ANY] * 4,
        out_specs=VMEM,
        scratch_shapes=[pltpu.VMEM((8, L), jnp.int32), pltpu.VMEM((L, L), BF), dma((6,))],
        compiler_params=pltpu.CompilerParams(vmem_limit_bytes=4194304),
        name="pack",
    )(*[pltpu.with_memory_space_constraint(v, pltpu.HBM) for v in (partners.reshape(8, L), k, x, y)])
    got = lax.all_to_all(sent, TMPL, 0, 0, tiled=True)
    repeated = pl.pallas_call(
        relay_kernel,
        out_shape=jax.ShapeDtypeStruct((128, 8, L), BF),
        in_specs=[SMEM, VMEM],
        out_specs=VMEM,
        compiler_params=SMALL,
        name="relay",
    )(owners, got)
    rev, ahead = pl.pallas_call(
        prepare_kernel,
        out_shape=(
            jax.ShapeDtypeStruct((2, L, L), F32),
            jax.ShapeDtypeStruct((2, 1280, 256), BF),
        ),
        in_specs=[SMEM, VMEM, ANY],
        out_specs=(VMEM, VMEM),
        scratch_shapes=[pltpu.VMEM((16, 8, L), BF), dma((16,))],
        cost_estimate=pl.CostEstimate(flops=10**7, bytes_accessed=10**6, transcendentals=0),
        compiler_params=SMALL,
        name="prepare",
    )(partners, k, got)
    whole = lax.all_to_all(repeated, ("trial",) + TMPL, 0, 0, tiled=True)
    out = pl.pallas_call(
        correlate_kernel,
        out_shape=jax.ShapeDtypeStruct((2, 16, 16384), BF),
        in_specs=[SMEM, SMEM, VMEM, VMEM, VMEM],
        out_specs=ANY,
        scratch_shapes=[
            pltpu.VMEM((2, 512, L), F32),
            pltpu.VMEM((136, L), F32),
            pltpu.VMEM((512, 1280), BF),
            pltpu.VMEM((512, 1280), BF),
            pltpu.VMEM((2, 1280, 256), BF),
            pltpu.VMEM((8, 1280, 256), BF),
            pltpu.VMEM((4096, L), F32),
            pltpu.VMEM((2, 16, 16384), BF),
            dma((8,)),
        ],
        compiler_params=LARGE,
        name="correlate",
    )(counts, owners, whole, rev, ahead)
    return out[:, None]


def solution(mesh):
    finer = Mesh(
        mesh.devices.reshape(mesh.shape["trial"], 4, 4, 4), ("trial", "tmpl_0", "tmpl_1", "tmpl_2")
    )
    in_specs = (
        P(None, "trial", TMPL, None, None),
        P(None, "trial", TMPL, None, None),
        P(TMPL, None, None),
        P(),
        P(),
        P(),
    )
    out_specs = P(None, "trial", TMPL, None)
    return jax.shard_map(body, mesh=finer, in_specs=in_specs, out_specs=out_specs, check_vma=False)
```

```python
import jax
import jax.numpy as jnp
from jax import lax
from jax.experimental import pallas as pl
from jax.experimental.pallas import tpu as pltpu
from jax.sharding import Mesh
from jax.sharding import PartitionSpec as P

TMPL = ("tmpl_0", "tmpl_1", "tmpl_2")
F32 = jnp.float32
BF = jnp.bfloat16
L = 128
VMEM = pl.BlockSpec(memory_space=pltpu.VMEM)
SMEM = pl.BlockSpec(memory_space=pltpu.SMEM)
ANY = pl.BlockSpec(memory_space=pl.ANY)
SMALL = pltpu.CompilerParams(vmem_limit_bytes=4 << 20)
LARGE = pltpu.CompilerParams(vmem_limit_bytes=24 << 20)


def iota(shape, axis):
    return lax.broadcasted_iota(jnp.int32, shape, axis)


def dot(a, b):
    return jnp.dot(a, b, preferred_element_type=F32)


def pack_kernel(part_hbm, k_hbm, x_ref, y_ref, buf, rev_ref, part_ref, k_ref, sems):
    me = lax.axis_index(TMPL)
    tables = (
        pltpu.make_async_copy(part_hbm, part_ref, sems.at[4]),
        pltpu.make_async_copy(k_hbm, k_ref, sems.at[5]),
    )
    for table in tables:
        table.start()
    loads = []
    for w in range(2):
        rows = slice(8 + 8 * w, 16 + 8 * w)
        loads.append(pltpu.make_async_copy(x_ref.at[w], buf.at[0:33, rows, :], sems.at[2 * w]))
        loads.append(pltpu.make_async_copy(y_ref.at[w], buf.at[33:50, rows, :], sems.at[2 * w + 1]))
    for load in loads:
        load.start()
    buf[50:64, 8:24, :] = jnp.zeros((14, 16, L), BF)
    group = (iota((64, L), 0) // 8 == iota((64, L), 1) // 16).astype(BF)
    same = iota((64, L), 0) % 8 == iota((64, L), 1) % 8
    for table in tables:
        table.wait()
    wanted = jnp.concatenate(
        [
            (jnp.broadcast_to(part_ref[r : r + 1, :], (L, L)) == me * 16 + iota((L, L), 0) // 8).astype(BF)
            for r in range(8)
        ],
        axis=0,
    )
    flip = (iota((L, L), 0) == (L - iota((L, L), 1)) % L).astype(BF)
    rev = dot(k_ref[...], flip).astype(BF)
    rev_ref[...] = rev
    hit = lax.dot_general(group, wanted, (((1,), (1,)), ((), ())), preferred_element_type=F32)
    pick = jnp.concatenate(
        [jnp.where(same, hit[:, r * L : (r + 1) * L], 0.0).astype(BF) for r in range(8)], axis=0
    )
    buf[:, 0:8, :] = dot(pick, rev).reshape(64, 8, L).astype(BF)
    for load in loads:
        load.wait()


def relay_kernel(owners_ref, part_ref, own_ref, got_ref, out_ref, rev_ref):
    me = lax.axis_index(TMPL)
    row = lax.axis_index("trial")
    for dest in range(2):
        w = jnp.where(owners_ref[0, dest] // 64 == row, 0, 1)
        start = pl.multiple_of(8 + 8 * w, 8)
        block = got_ref[owners_ref[w, dest] % 64, pl.ds(start, 8), :]
        out_ref[64 * dest : 64 * dest + 64] = jnp.broadcast_to(block[None], (64, 8, L))
    rev_ref[0] = own_ref[...].astype(F32)
    for s in range(16):
        source = jnp.maximum(part_ref[me * 16 + s], 0) // 16
        rev_ref[1, 8 * s : 8 * s + 8, :] = got_ref[source, 0:8, :].astype(F32)


class Taps:
    def __init__(self, rev_ref):
        self.rev = rev_ref
        self.tri = iota((L, L), 0) >= iota((L, L), 1)
        self.tri_half = iota((L, L), 0) >= iota((L, L), 1) % 64
        self.left = iota((L, L), 1) < 64
        self.zero = jnp.zeros((L, L), F32)

    def circulant(self, kind, row, shift):
        v = jnp.broadcast_to(self.rev[kind, pl.ds(row, 1), :], (L, L))
        return pltpu.roll(v, shift, 1, stride=1, stride_axis=0)

    def put(self, dst, c, side, cs, mask):
        lower = cs + [self.zero]
        upper = [self.zero] + cs
        for q in range(5):
            tile = jnp.where(mask, lower[q], upper[q]).astype(BF)
            dst[(5 * c + q) * L : (5 * c + q + 1) * L, side * L : (side + 1) * L] = tile

    def direct(self, pair, dst):
        for k in range(2):
            for c in range(2):
                row = (2 * pair + k) * 8 + c
                self.put(dst, c, k, [self.circulant(0, row + 2 * q, 0) for q in range(4)], self.tri)

    def plane(self, group, dst):
        for k in range(2):
            for c in range(2):
                row = (4 * group + 2 * k) * 8 + c
                both = [
                    jnp.where(self.left, self.circulant(1, row + 2 * q, 0), self.circulant(1, row + 8 + 2 * q, 64))
                    for q in range(4)
                ]
                self.put(dst, c, k, both, self.tri_half)


def correlate_kernel(
    counts_ref, owners_ref, whole, rev_ref, out_ref, flat, y64, lx, ly, rp, rd, scr, obuf, sems
):
    me = lax.axis_index(TMPL)
    live_n = counts_ref[me]
    taps = Taps(rev_ref)

    dup = (iota((L, 2 * L), 0) == (iota((L, 2 * L), 1) // L) * 64 + (iota((L, 2 * L), 1) % L) // 2).astype(BF)

    def power(rows, w, operand):
        z = dot(rows[256 * w : 256 * w + 256, :], operand[...])
        return z[:L] * z[:L] + z[L:] * z[L:]

    def finish(pair, w, plane):
        wide = dot(plane[:, (pair % 2) * L : (pair % 2 + 1) * L], dup)
        total = power(lx, w, rd.at[pair]) + wide
        for j in range(2):
            t = 2 * pair + j
            rows = pl.ds(w * 2048 + t, L, stride=16)
            scr[rows, :] = jnp.where(t < live_n, total[:, j * L : (j + 1) * L], 0.0)

    stores = []

    def merge(w):
        for part in range(4):
            for a in range(32 * part, 32 * part + 32):
                rows = slice((w * L + a) * 16, (w * L + a + 1) * 16)
                obuf[w, :, a * L : (a + 1) * L] = scr[rows, :].astype(BF)
            cols = slice(part * 4096, (part + 1) * 4096)
            copy = pltpu.make_async_copy(obuf.at[w, :, cols], out_ref.at[w, :, cols], sems.at[4 * w + part])
            copy.start()
            stores.append(copy)

    taps.plane(0, rp.at[0])
    taps.plane(1, rp.at[1])
    lane = iota((68, L), 1)
    for w in range(2):
        held = owners_ref[w, lax.axis_index("trial")] // 64
        flat[w] = whole[pl.ds(64 * held, 64)].astype(F32).reshape(512, L)
        top, low = slice(256 * w, 256 * w + L), slice(256 * w + L, 256 * w + 256)
        for c in range(2):
            even = flat[w, pl.ds(264 + c, 68, stride=2), :]
            after = flat[w, pl.ds(266 + c, 68, stride=2), :]
            y64[pl.ds(0, 68, stride=2), :] = even
            y64[pl.ds(1, 68, stride=2), :] = jnp.where(lane < 64, pltpu.roll(even, 64, 1), pltpu.roll(after, 64, 1))
            for q in range(5):
                here = slice((5 * c + q) * L, (5 * c + q + 1) * L)
                there = slice((5 - 5 * c + q) * L, (6 - 5 * c + q) * L)
                for dst, v in (
                    (lx, flat[w, pl.ds(2 * q + c, L, stride=2), :]),
                    (ly, y64[2 * q : 2 * q + L, :]),
                ):
                    dst[top, here] = (v if c == 0 else -v).astype(BF)
                    dst[low, there] = v.astype(BF)

    for half in range(2):
        pairs = range(4 * half, 4 * half + 4)
        taps.direct(pairs[0], rd.at[pairs[0]])
        taps.direct(pairs[1], rd.at[pairs[1]])
        planes = [[power(ly, w, rp.at[2 * half + k]).astype(BF) for w in range(2)] for k in range(2)]
        taps.direct(pairs[2], rd.at[pairs[2]])
        taps.direct(pairs[3], rd.at[pairs[3]])
        if half == 0:
            for pair in pairs:
                if pair == 2:
                    taps.plane(2, rp.at[2])
                    taps.plane(3, rp.at[3])
                for w in range(2):
                    finish(pair, w, planes[pair // 2 % 2][w])
        else:
            for w in range(2):
                for pair in pairs:
                    finish(pair, w, planes[pair // 2 % 2][w])
                merge(w)
    for store in stores:
        store.wait()


def body(spectra, half_spectra, kernels, owners, counts, partners):
    x = spectra.reshape(2, 2, 33, 4, L).transpose(0, 2, 3, 1, 4).reshape(2, 33, 8, L)
    y = half_spectra.reshape(2, 2, 17, 4, L).transpose(0, 2, 3, 1, 4).reshape(2, 17, 8, L)
    k = kernels.reshape(16, 2, 4, L).transpose(0, 2, 1, 3).reshape(L, L)
    dma = pltpu.SemaphoreType.DMA
    sent, own = pl.pallas_call(
        pack_kernel,
        out_shape=(jax.ShapeDtypeStruct((64, 24, L), BF), jax.ShapeDtypeStruct((L, L), BF)),
        in_specs=[ANY] * 4,
        out_specs=(VMEM, VMEM),
        scratch_shapes=[pltpu.VMEM((8, L), jnp.int32), pltpu.VMEM((L, L), BF), dma((6,))],
        compiler_params=pltpu.CompilerParams(vmem_limit_bytes=4194304),
        name="pack",
    )(*[pltpu.with_memory_space_constraint(v, pltpu.HBM) for v in (partners.reshape(8, L), k, x, y)])
    got = lax.all_to_all(sent, TMPL, 0, 0, tiled=True)
    repeated, rev = pl.pallas_call(
        relay_kernel,
        out_shape=(jax.ShapeDtypeStruct((128, 8, L), BF), jax.ShapeDtypeStruct((2, L, L), F32)),
        in_specs=[SMEM, SMEM, VMEM, VMEM],
        out_specs=(VMEM, VMEM),
        compiler_params=SMALL,
        name="relay",
    )(*[pltpu.with_memory_space_constraint(v, pltpu.HBM) for v in (owners, partners)], own, got)
    whole = lax.all_to_all(repeated, ("trial",) + TMPL, 0, 0, tiled=True)
    out = pl.pallas_call(
        correlate_kernel,
        out_shape=jax.ShapeDtypeStruct((2, 16, 16384), BF),
        in_specs=[SMEM, SMEM, VMEM, VMEM],
        out_specs=ANY,
        scratch_shapes=[
            pltpu.VMEM((2, 512, L), F32),
            pltpu.VMEM((136, L), F32),
            pltpu.VMEM((512, 1280), BF),
            pltpu.VMEM((512, 1280), BF),
            pltpu.VMEM((4, 1280, 256), BF),
            pltpu.VMEM((8, 1280, 256), BF),
            pltpu.VMEM((4096, L), F32),
            pltpu.VMEM((2, 16, 16384), BF),
            dma((8,)),
        ],
        compiler_params=LARGE,
        name="correlate",
    )(*[pltpu.with_memory_space_constraint(v, pltpu.HBM) for v in (counts, owners)], whole, rev)
    return out[:, None]


def solution(mesh):
    finer = Mesh(
        mesh.devices.reshape(mesh.shape["trial"], 4, 4, 4), ("trial", "tmpl_0", "tmpl_1", "tmpl_2")
    )
    in_specs = (
        P(None, "trial", TMPL, None, None),
        P(None, "trial", TMPL, None, None),
        P(TMPL, None, None),
        P(),
        P(),
        P(),
    )
    out_specs = P(None, "trial", TMPL, None)
    return jax.shard_map(body, mesh=finer, in_specs=in_specs, out_specs=out_specs, check_vma=False)
```
